256 devices in a mesh: tok: 32 (over x, z), head: 8 (over y, core).
Axes of the slice: x: 4, y: 4, z: 8, core: 2. Of those that a mesh axis runs over, the one named last changes fastest.
Arguments:
- queries: bfloat16 [131072, 8, 1024], P('tok', 'head'), as said below
- keys: bfloat16 [131072, 8, 128], P('tok', 'head'), as said below
- basis: float32 [8, 1024, 256], P('head'), may hold values from -0.1875 to 0.1875
Outputs:
- subspace: float32 [8, 1024, 256], P('head')
- keymap: float32 [8, 128, 256], replicated
The draws below stay inside these ranges and needn't reach their ends.
Inputs may be any that keep to these rules, and one draw needn't show every extreme that they name: `queries`: query features are correlated within a group and share a common part with the keys. `keys`: keys share a common part with the queries of the same tokens.
All inputs are finite; a program needn't handle non-finite values.
Results may differ from the reference program's by a relative error of at most 0.0007.
Values sent between devices are 32-bit elements; how exact they have to be, the bound alone decides.
No kernel may reach another device: no remote copies, remote signals or barrier semaphores. Data moves between devices by JAX's collectives and lax.ppermute only.
A program may use at most 64 MiB of HBM per device.

```python
import math
import jax
import jax.numpy as jnp
from jax import lax

HD = 128
RANK = 256
GROUPS = 8
QW = 1024
TOKENS = 131072


def shared_part(key):
    latent = jax.random.normal(jax.random.fold_in(key, 7), (TOKENS, 16), jnp.float32)
    rowscale = jnp.exp(jax.random.uniform(jax.random.fold_in(key, 8), (TOKENS, 1, 1), jnp.float32) * math.log(10.0))
    return (latent, rowscale)


def draw_queries(key, part):
    latent, rowscale = shared_part(key)
    noise = jax.random.normal(jax.random.fold_in(key, 1), (TOKENS, GROUPS, QW), jnp.float32)
    colscale = jnp.exp(jax.random.uniform(jax.random.fold_in(key, 3), (1, GROUPS, QW), jnp.float32) * math.log(3.0))
    spread = jnp.repeat(latent, QW // 16, axis=-1)[:, None, :]
    mixed = noise + 0.6 * jnp.roll(noise, 1, axis=-1) + 0.7 * spread
    return (0.5 * mixed * colscale * rowscale).astype(jnp.bfloat16)


def draw_keys(key, part):
    latent, rowscale = shared_part(key)
    noise = jax.random.normal(jax.random.fold_in(key, 4), (TOKENS, GROUPS, HD), jnp.float32)
    spread = jnp.repeat(latent, HD // 16, axis=-1)[:, None, :]
    return ((0.6 * noise + spread) * rowscale * 0.5).astype(jnp.bfloat16)


def levels(key, shape, shards, low, top_value):
    factor_of, own = 1.0, jax.random.fold_in(key, 6)
    for dim, blocks in shards:
        steps = jnp.exp(jax.random.uniform(jax.random.fold_in(own, dim), (blocks,), jnp.float32, low / len(shards), top_value / len(shards)))
        factor_of = factor_of * jnp.repeat(steps, shape[dim] // blocks).reshape([-1 if axis == dim else 1 for axis in range(len(shape))])
    return factor_of


def centred(own_key, shape, scale, bound, pieces=(), held_as=jnp.bfloat16):
    loudness = levels(own_key, shape, pieces, -0.22, 0.18) if pieces else 1.0
    array = jax.random.normal(own_key, shape, jnp.float32) * scale * loudness
    return jnp.minimum(jnp.maximum(array, -bound), bound).astype(held_as)


def setup_inputs(seed: int = 0) -> dict:
    streams_of = jax.random.split(jax.random.key(seed), 4)
    return {
        "queries": draw_queries(jax.random.fold_in(streams_of[3], 71), 0),
        "keys": draw_keys(jax.random.fold_in(streams_of[3], 71), 0),
        "basis": centred(streams_of[2], (GROUPS, QW, RANK), QW ** -0.5, 0.1875, ((0, 8),), jnp.float32),
    }


ridge = 0.1
eps = 1e-06
high = lax.Precision.HIGHEST

def orthonormal(image):
    inner = jnp.dot(image.T, image, precision=high)
    lower = jnp.linalg.cholesky(inner)
    return jax.scipy.linalg.solve_triangular(lower, image.T, lower=True).T

def solve_group(query_rows, key_rows, start_basis):
    gram = jnp.dot(query_rows.T.astype(jnp.float32), query_rows.astype(jnp.float32), preferred_element_type=jnp.float32) / TOKENS
    cross = jnp.dot(key_rows.T.astype(jnp.float32), query_rows.astype(jnp.float32), preferred_element_type=jnp.float32) / TOKENS
    scale = jnp.trace(gram) / gram.shape[0] + eps
    image = jnp.dot(gram, start_basis, precision=high)
    refined = orthonormal(image)
    small = jnp.dot(refined.T, jnp.dot(gram, refined, precision=high), precision=high)
    reduced = small / scale + ridge * jnp.eye(refined.shape[1], dtype=jnp.float32)
    rhs = jnp.dot(cross, refined, precision=high)
    factor = jnp.linalg.cholesky(reduced)
    mapped = jax.scipy.linalg.cho_solve((factor, True), rhs.T).T
    return (refined, mapped)

def reference(queries, keys, basis):
    spaces = []
    maps = []
    for group in range(GROUPS):
        refined, mapped = solve_group(queries[:, group, :], keys[:, group, :], basis[group])
        spaces.append(refined)
        maps.append(mapped)
    return (jnp.stack(spaces), jnp.stack(maps))
```

```python
import jax
import jax.numpy as jnp
from jax import lax
from jax.experimental import pallas as pl
from jax.experimental.pallas import tpu as pltpu
from jax.sharding import PartitionSpec as P

ridge = 0.1
eps = 1e-06
high = lax.Precision.HIGHEST
f32 = jnp.float32

NX, NZ, NY, NCORE = 4, 8, 4, 2

VMEM_LIMIT = 48 * 1024 * 1024


def dot(a, b, ca, cb, precision=high):
    return lax.dot_general(
        a, b, (((ca,), (cb,)), ((), ())), precision=precision, preferred_element_type=f32
    )


def call(body, outs, scratch, *args, scalars=1):
    spec = pl.BlockSpec(memory_space=pltpu.VMEM)
    small = pl.BlockSpec(memory_space=pltpu.SMEM)
    many = isinstance(outs, list)
    shapes = [jax.ShapeDtypeStruct(s, f32) for s in (outs if many else [outs])]
    result = pl.pallas_call(
        body,
        out_shape=shapes,
        in_specs=[small] * scalars + [spec] * (len(args) - scalars),
        out_specs=[spec] * len(shapes),
        scratch_shapes=scratch,
        compiler_params=pltpu.CompilerParams(vmem_limit_bytes=VMEM_LIMIT),
    )(*args)
    return result if many else result[0]


def inverse_factor_128(read, write):
    tile = (8, 128)
    row = lax.broadcasted_iota(jnp.int32, tile, 0)
    lane = lax.broadcasted_iota(jnp.int32, tile, 1)
    left = [read(r) for r in range(16)]
    right = [jnp.where(lane == row + 8 * r, 1.0, 0.0).astype(f32) for r in range(16)]

    def lanes(v, j):
        return jnp.broadcast_to(v[:, j : j + 1], tile)

    def rows(v, i):
        return jnp.broadcast_to(v[i : i + 1, :], tile)

    for p in range(16):
        base = 8 * p
        cols = [lanes(left[p], base + j) for j in range(8)]
        s = [[rows(cols[j], i) for j in range(i + 1)] for i in range(8)]
        inv = [[None] * 8 for _ in range(8)]
        for j in range(8):
            r = lax.rsqrt(s[j][j])
            inv[j][j] = r
            c = {i: s[i][j] * r for i in range(j + 1, 8)}
            for i in range(j + 1, 8):
                for l in range(j + 1, i + 1):
                    s[i][l] = s[i][l] - c[i] * c[l]
                s[i][j] = c[i]
        for i in range(1, 8):
            for j in range(i):
                t = s[i][j] * inv[j][j]
                for l in range(j + 1, i):
                    t = t + s[i][l] * inv[l][j]
                inv[i][j] = -(t * inv[i][i])
        dl = [rows(left[p], i) for i in range(8)]
        dr = [rows(right[p], i) for i in range(8)]
        ul, ur = [], []
        for i in range(8):
            a = inv[i][0] * dl[0]
            b = inv[i][0] * dr[0]
            for j in range(1, i + 1):
                a = a + inv[i][j] * dl[j]
                b = b + inv[i][j] * dr[j]
            ul.append(a)
            ur.append(b)
        out = ur[0]
        for i in range(1, 8):
            out = jnp.where(row == i, ur[i], out)
        write(p, out)
        for k in range(p + 1, 16):
            a = [lanes(left[k], base + j) for j in range(8)]
            for i in range(8):
                c = inv[i][0] * a[0]
                for j in range(1, i + 1):
                    c = c + inv[i][j] * a[j]
                left[k] = left[k] - c * ul[i]
                right[k] = right[k] - c * ur[i]


def inverse_factor_256(a_ref, li_ref):
    def top(r, v):
        li_ref[8 * r : 8 * r + 8, 0:128] = v

    def bottom(r, v):
        li_ref[128 + 8 * r : 136 + 8 * r, 128:256] = v

    inverse_factor_128(lambda r: a_ref[8 * r : 8 * r + 8, 0:128], top)
    li11 = li_ref[0:128, 0:128]
    l21 = dot(a_ref[128:256, 0:128], li11, 1, 1)
    a_ref[128:256, 128:256] = a_ref[128:256, 128:256] - dot(l21, l21, 1, 1)
    inverse_factor_128(lambda r: a_ref[128 + 8 * r : 136 + 8 * r, 128:256], bottom)
    li22 = li_ref[128:256, 128:256]
    li_ref[128:256, 0:128] = -dot(li22, dot(l21, li11, 1, 0), 1, 0)
    li_ref[0:128, 128:256] = jnp.zeros((128, 128), f32)


def local_products(norm, pos, q_ref, k_ref, b_ref, gram, cross, o0, o1, o2, o3):
    step = pl.program_id(0)

    @pl.when(step == 0)
    def _():
        gram[...] = jnp.zeros_like(gram)
        cross[...] = jnp.zeros_like(cross)

    for i in range(4):
        lo, hi = 256 * i, 256 * i + 256
        gram[lo:hi, lo:] += dot(q_ref[:, lo:hi], q_ref[:, lo:], 0, 0, None)
    cross[...] += dot(k_ref[...], q_ref[...], 0, 0, None)

    @pl.when(step == pl.num_programs(0) - 1)
    def _():
        for i in range(4):
            for j in range(i, 4):
                block = gram[256 * i : 256 * i + 256, 256 * j : 256 * j + 256] * norm
                gram[256 * i : 256 * i + 256, 256 * j : 256 * j + 256] = block
                if j > i:
                    gram[256 * j : 256 * j + 256, 256 * i : 256 * i + 256] = block.T
        cross[...] = cross[...] * norm
        basis = b_ref[...]
        for k, out in enumerate((o0, o1, o2, o3)):
            start = pl.multiple_of(lax.rem(pos[0] + k, NX) * 256, 256)
            out[...] = dot(gram[pl.ds(start, 256), :], basis, 1, 0)


def products_call(pos, q, k, b, total):
    tokens, width = q.shape
    tile = 1024
    whole = lambda shape: pl.BlockSpec(shape, lambda i, p: (0,) * len(shape))
    rank = b.shape[1]
    out_shapes = [(width, width), (k.shape[1], width)] + [(width // NX, rank)] * NX

    def body(*refs):
        local_products(1.0 / total, *refs)

    return pl.pallas_call(
        body,
        out_shape=[jax.ShapeDtypeStruct(s, f32) for s in out_shapes],
        grid_spec=pltpu.PrefetchScalarGridSpec(
            num_scalar_prefetch=1,
            grid=(tokens // tile,),
            in_specs=[
                pl.BlockSpec((tile, width), lambda i, p: (i, 0)),
                pl.BlockSpec((tile, k.shape[1]), lambda i, p: (i, 0)),
                whole(b.shape),
            ],
            out_specs=[whole(s) for s in out_shapes],
        ),
        compiler_params=pltpu.CompilerParams(vmem_limit_bytes=VMEM_LIMIT),
    )(pos, q, k, b)


def sum_and_split(pos, a0, a1, a2, a3, *rest):
    outs, acc = rest[:NZ], rest[NZ]
    acc[...] = (a0[...] + a2[...]) + (a1[...] + a3[...])
    size = acc.shape[0] // NZ
    for k, out in enumerate(outs):
        start = pl.multiple_of(lax.rem(pos[1] + k, NZ) * size, size)
        out[...] = acc[pl.ds(start, size), :]


def join(pos, *refs):
    blocks, out = refs[:NZ], refs[NZ]
    size = blocks[0].shape[0]
    for k, block in enumerate(blocks):
        start = pl.multiple_of(lax.rem(pos[1] + NZ - k, NZ) * size, size)
        out[pl.ds(start, size), :] = block[...]


def subspace_body(pos, s0, s1, s2, s3, gram, cross, refined, packed, image, inner, li):
    for k, block in enumerate((s0, s1, s2, s3)):
        start = pl.multiple_of(lax.rem(pos[0] + NX - k, NX) * 256, 256)
        image[pl.ds(start, 256), :] = block[...]
    inner[...] = dot(image[...], image[...], 0, 0)
    inverse_factor_256(inner, li)
    refined[...] = dot(image[...], li[...], 1, 1)
    basis = refined[...]
    product = dot(gram[...], basis, 1, 0)
    small = dot(basis, product, 0, 0)
    size = 256
    row = lax.broadcasted_iota(jnp.int32, (size, size), 0)
    col = lax.broadcasted_iota(jnp.int32, (size, size), 1)
    diagonal = jnp.zeros((size, size), f32)
    for i in range(4):
        block = gram[256 * i : 256 * i + 256, 256 * i : 256 * i + 256]
        diagonal = diagonal + jnp.where(row == col, block, 0.0)
    trace = jnp.sum(jnp.sum(diagonal, axis=1, keepdims=True), axis=0, keepdims=True)
    packed[0:128, 0:128] = small[0:128, 0:128]
    packed[0:128, 128:256] = jnp.broadcast_to(trace, (128, 128))
    packed[128:256, :] = small[128:256, :]
    packed[256:384, :] = dot(cross[...], basis, 1, 0)


def keymap_body(width, pos, *refs):
    blocks, out, joined, reduced, li = refs[:NZ], refs[NZ], refs[NZ + 1], refs[NZ + 2], refs[NZ + 3]
    join(pos, *blocks, joined)
    scale = joined[0:1, 128:129] / width + eps
    row = lax.broadcasted_iota(jnp.int32, (256, 256), 0)
    col = lax.broadcasted_iota(jnp.int32, (256, 256), 1)
    identity = jnp.where(row == col, ridge, 0.0).astype(f32)
    reduced[...] = joined[0:256, :] / scale + identity
    inverse_factor_256(reduced, li)
    out[...] = dot(dot(joined[256:384, :], li[...], 1, 1), li[...], 1, 0)


def place_body(pos, own, other, out):
    for k in range(NY):
        y = lax.rem(pos[2] + NY - k, NY)
        out[NCORE * y + pos[3]] = own[128 * k : 128 * k + 128, :]
        out[NCORE * y + (1 - pos[3])] = other[128 * k : 128 * k + 128, :]


def along_x(value, k):
    pairs = [(x * NZ + z, ((x + k) % NX) * NZ + z) for x in range(NX) for z in range(NZ)]
    return lax.ppermute(value, "tok", pairs)


def along_z(value, k):
    pairs = [(x * NZ + z, x * NZ + (z + k) % NZ) for x in range(NX) for z in range(NZ)]
    return lax.ppermute(value, "tok", pairs)


def along_y(value, k):
    pairs = [(y * NCORE + c, ((y + k) % NY) * NCORE + c) for y in range(NY) for c in range(NCORE)]
    return lax.ppermute(value, "head", pairs)


def other_core(value):
    pairs = [(y * NCORE + c, y * NCORE + 1 - c) for y in range(NY) for c in range(NCORE)]
    return lax.ppermute(value, "head", pairs)


def reduce_along_z(pos, parts):
    rows, cols = parts[0].shape
    block = (rows // NZ, cols)
    pieces = call(sum_and_split, [block] * NZ, [pltpu.VMEM((rows, cols), f32)], pos, *parts)
    total = pieces[0]
    for k in range(1, NZ):
        total = total + along_z(pieces[k], k)
    return [total] + [along_z(total, k) for k in range(1, NZ)]


def on_device(queries, keys, basis):
    q, key, b = queries[:, 0, :], keys[:, 0, :], basis[0]
    width, rank = b.shape
    features = key.shape[1]
    total = q.shape[0] * lax.axis_size("tok")
    tok, head = lax.axis_index("tok"), lax.axis_index("head")
    pos = jnp.stack([tok // NZ, tok % NZ, head // NCORE, head % NCORE]).astype(jnp.int32)

    gram, cross, *image_parts = products_call(pos, q, key, b, total)
    arrived = [image_parts[0]] + [along_x(image_parts[k], k) for k in range(1, NX)]
    blocks = reduce_along_z(pos, arrived)
    rows = call(join, (width // NX, rank), [], pos, *blocks)
    quarters = [rows] + [along_x(rows, k) for k in range(1, NX)]

    square = pltpu.VMEM((rank, rank), f32)
    refined, packed = call(
        subspace_body,
        [(width, rank), (rank + features, rank)],
        [pltpu.VMEM((width, rank), f32), square, square],
        pos, *quarters, gram, cross,
    )
    arrived = [packed] + [along_x(packed, k) for k in range(1, NX)]
    blocks = reduce_along_z(pos, arrived)

    def keymap(*refs):
        keymap_body(width, *refs)

    mapped = call(
        keymap,
        (features, rank),
        [pltpu.VMEM((rank + features, rank), f32), square, square],
        pos, *blocks,
    )
    own = jnp.concatenate([mapped] + [along_y(mapped, k) for k in range(1, NY)], axis=0)
    every_map = call(
        place_body, (NY * NCORE, features, rank), [], pos, own, other_core(own)
    )
    return refined[None], every_map


def solution(mesh):
    placed = (P("tok", "head", None), P("tok", "head", None), P("head", None, None))
    return jax.shard_map(
        on_device,
        mesh=mesh,
        in_specs=placed,
        out_specs=(P("head", None, None), P()),
        check_vma=False,
    )
```

```python
import jax
import jax.numpy as jnp
from jax import lax
from jax.experimental import pallas as pl
from jax.experimental.pallas import tpu as pltpu
from jax.sharding import PartitionSpec as P

ridge = 0.1
eps = 1e-06
high = lax.Precision.HIGHEST
f32 = jnp.float32
bf16 = jnp.bfloat16

NX, NZ, NY, NCORE = 4, 8, 4, 2
NQ = 4

VMEM_LIMIT = 48 * 1024 * 1024


def dot(a, b, ca, cb, precision=high):
    return lax.dot_general(
        a, b, (((ca,), (cb,)), ((), ())), precision=precision, preferred_element_type=f32
    )


def split(v):
    top = v.astype(bf16)
    return top, (v - top.astype(f32)).astype(bf16)


def dot_split(a, b, ca, cb):
    (ah, al), (bh, bl) = a, b
    return dot(ah, bh, ca, cb, None) + (dot(ah, bl, ca, cb, None) + dot(al, bh, ca, cb, None))


def call(body, outs, scratch, pos, *args, far=()):
    spec = pl.BlockSpec(memory_space=pltpu.VMEM)
    hbm = pl.BlockSpec(memory_space=pltpu.HBM)
    many = isinstance(outs, list)
    shapes = [jax.ShapeDtypeStruct(s, f32) for s in (outs if many else [outs])]
    in_specs = [pl.BlockSpec(memory_space=pltpu.SMEM)] + [spec] * len(args) + [hbm] * len(far)
    args = (pos, *args, *far)
    result = pl.pallas_call(
        body,
        out_shape=shapes,
        in_specs=in_specs,
        out_specs=[spec] * len(shapes),
        scratch_shapes=scratch,
        compiler_params=pltpu.CompilerParams(vmem_limit_bytes=VMEM_LIMIT),
    )(*args)
    return result if many else result[0]


def inverse_factor_128(read, write):
    tile = (8, 128)
    row = lax.broadcasted_iota(jnp.int32, tile, 0)
    lane = lax.broadcasted_iota(jnp.int32, tile, 1)
    left = [read(r) for r in range(16)]
    right = [jnp.where(lane == row + 8 * r, 1.0, 0.0).astype(f32) for r in range(16)]

    def lanes(v, j):
        return jnp.broadcast_to(v[:, j : j + 1], tile)

    def rows(v, i):
        return jnp.broadcast_to(v[i : i + 1, :], tile)

    for p in range(16):
        base = 8 * p
        cols = [lanes(left[p], base + j) for j in range(8)]
        s = [[rows(cols[j], i) for j in range(i + 1)] for i in range(8)]
        inv = [[None] * 8 for _ in range(8)]
        for j in range(8):
            r = lax.rsqrt(s[j][j])
            inv[j][j] = r
            c = {i: s[i][j] * r for i in range(j + 1, 8)}
            for i in range(j + 1, 8):
                for l in range(j + 1, i + 1):
                    s[i][l] = s[i][l] - c[i] * c[l]
                s[i][j] = c[i]
        for i in range(1, 8):
            for j in range(i):
                t = s[i][j] * inv[j][j]
                for l in range(j + 1, i):
                    t = t + s[i][l] * inv[l][j]
                inv[i][j] = -(t * inv[i][i])
        dl = [rows(left[p], i) for i in range(8)]
        dr = [rows(right[p], i) for i in range(8)]
        ul, ur = [], []
        for i in range(8):
            a = inv[i][0] * dl[0]
            b = inv[i][0] * dr[0]
            for j in range(1, i + 1):
                a = a + inv[i][j] * dl[j]
                b = b + inv[i][j] * dr[j]
            ul.append(a)
            ur.append(b)
        out = ur[0]
        for i in range(1, 8):
            out = jnp.where(row == i, ur[i], out)
        write(p, out)
        for k in range(p + 1, 16):
            a = [lanes(left[k], base + j) for j in range(8)]
            for i in range(8):
                c = inv[i][0] * a[0]
                for j in range(1, i + 1):
                    c = c + inv[i][j] * a[j]
                left[k] = left[k] - c * ul[i]
                right[k] = right[k] - c * ur[i]


def inverse_factor_256(a_ref, li_ref):
    def top(r, v):
        li_ref[8 * r : 8 * r + 8, 0:128] = v

    def bottom(r, v):
        li_ref[128 + 8 * r : 136 + 8 * r, 128:256] = v

    inverse_factor_128(lambda r: a_ref[8 * r : 8 * r + 8, 0:128], top)
    li11 = li_ref[0:128, 0:128]
    l21 = dot(a_ref[128:256, 0:128], li11, 1, 1)
    a_ref[128:256, 128:256] = a_ref[128:256, 128:256] - dot(l21, l21, 1, 1)
    inverse_factor_128(lambda r: a_ref[128 + 8 * r : 136 + 8 * r, 128:256], bottom)
    li22 = li_ref[128:256, 128:256]
    li_ref[128:256, 0:128] = -dot(li22, dot(l21, li11, 1, 0), 1, 0)
    li_ref[0:128, 128:256] = jnp.zeros((128, 128), f32)


def products_call(pos, q, k, b, total):
    tokens, width = q.shape
    features, rank = k.shape[1], b.shape[1]
    tiles = [tokens // 8, tokens // 8, tokens // 4, tokens // 2]
    edges = [sum(tiles[:i]) for i in range(len(tiles) + 1)]
    count = len(tiles)
    side = width // 4
    spans = [slice(side * i, side * i + side) for i in range(4)]
    norm = 1.0 / total

    def body(pos, q_hbm, k_hbm, b_hbm, top_hbm, low_hbm, cross, trace, o0, o1, o2, o3,
             q, k, b, gram, top, low, sems):
        arrivals = []
        for i in range(count):
            part = pl.ds(edges[i], tiles[i])
            pair = [
                pltpu.make_async_copy(q_hbm.at[part], q.at[part], sems.at[2 * i]),
                pltpu.make_async_copy(k_hbm.at[part], k.at[part], sems.at[2 * i + 1]),
            ]
            for copy in pair:
                copy.start()
            arrivals.append(pair)
        basis_copy = pltpu.make_async_copy(b_hbm, b, sems.at[2 * count])
        basis_copy.start()
        for i in range(count):
            for copy in arrivals[i]:
                copy.wait()
            rows = slice(edges[i], edges[i + 1])
            for span in spans:
                part = dot(q[rows, span], q[rows, span.start:], 0, 0, None)
                gram[span, span.start:] = part if i == 0 else gram[span, span.start:] + part
            part = dot(k[rows, :], q[rows, :], 0, 0, None)
            cross[...] = part if i == 0 else cross[...] + part
        cross[...] = cross[...] * norm

        row = lax.broadcasted_iota(jnp.int32, (side, side), 0)
        col = lax.broadcasted_iota(jnp.int32, (side, side), 1)
        diagonal = jnp.zeros((side, side), f32)
        for i in range(4):
            for j in range(i, 4):
                block = gram[spans[i], spans[j]] * norm
                top[spans[i], spans[j]], low[spans[i], spans[j]] = split(block)
                if j == i:
                    diagonal = diagonal + jnp.where(row == col, block, 0.0)
                else:
                    top[spans[j], spans[i]], low[spans[j], spans[i]] = split(block.T)
        total_of = jnp.sum(jnp.sum(diagonal, axis=1, keepdims=True), axis=0, keepdims=True)
        trace[...] = jnp.broadcast_to(total_of, trace.shape)

        top_copy = pltpu.make_async_copy(top, top_hbm, sems.at[2 * count + 1])
        low_copy = pltpu.make_async_copy(low, low_hbm, sems.at[2 * count + 2])
        top_copy.start()
        low_copy.start()
        basis_copy.wait()
        basis = split(b[...])
        for j, out in enumerate((o0, o1, o2, o3)):
            part = pl.ds(pl.multiple_of(lax.rem(pos[0] + j, NX) * side, side), side)
            out[...] = dot_split((top[part, :], low[part, :]), basis, 1, 0)
        top_copy.wait()
        low_copy.wait()

    hbm = pl.BlockSpec(memory_space=pltpu.HBM)
    vmem = pl.BlockSpec(memory_space=pltpu.VMEM)
    shape = jax.ShapeDtypeStruct
    return pl.pallas_call(
        body,
        out_shape=[
            shape((width, width), bf16),
            shape((width, width), bf16),
            shape((features, width), f32),
            shape((8, 128), f32),
        ] + [shape((side, rank), f32)] * NX,
        in_specs=[pl.BlockSpec(memory_space=pltpu.SMEM), hbm, hbm, hbm],
        out_specs=[hbm, hbm] + [vmem] * (2 + NX),
        scratch_shapes=[
            pltpu.VMEM((tokens, width), bf16),
            pltpu.VMEM((tokens, features), bf16),
            pltpu.VMEM((width, rank), f32),
            pltpu.VMEM((width, width), f32),
            pltpu.VMEM((width, width), bf16),
            pltpu.VMEM((width, width), bf16),
            pltpu.SemaphoreType.DMA((2 * count + 3,)),
        ],
        compiler_params=pltpu.CompilerParams(vmem_limit_bytes=VMEM_LIMIT),
    )(pos, q, k, b)


def sum_and_split(pos, a0, a1, a2, a3, o0, o1, o2, o3, acc):
    acc[...] = (a0[...] + a2[...]) + (a1[...] + a3[...])
    size = acc.shape[0] // NQ
    for j, out in enumerate((o0, o1, o2, o3)):
        start = pl.multiple_of(lax.rem(pos[1] + j, NQ) * size, size)
        out[...] = acc[pl.ds(start, size), :]


def join(pos, a0, a1, a2, a3, out):
    size = a0.shape[0]
    for j, block in enumerate((a0, a1, a2, a3)):
        start = pl.multiple_of(lax.rem(pos[1] + NQ - j, NQ) * size, size)
        out[pl.ds(start, size), :] = block[...]


def subspace_body(pos, s0, s1, s2, s3, cross, trace, top_hbm, low_hbm, refined, packed,
                  image, inner, li, top, low, sems):
    top_copy = pltpu.make_async_copy(top_hbm, top, sems.at[0])
    low_copy = pltpu.make_async_copy(low_hbm, low, sems.at[1])
    top_copy.start()
    low_copy.start()
    size = s0.shape[0]
    for j, block in enumerate((s0, s1, s2, s3)):
        start = pl.multiple_of(lax.rem(pos[0] + NX - j, NX) * size, size)
        image[pl.ds(start, size), :] = block[...]
    inner[...] = dot(image[...], image[...], 0, 0)
    inverse_factor_256(inner, li)
    basis = dot(image[...], li[...], 1, 1)
    refined[...] = basis
    parts = split(basis)
    top_copy.wait()
    low_copy.wait()
    product = dot_split((top[...], low[...]), parts, 1, 0)
    small = dot_split(parts, split(product), 0, 0)
    packed[:, 0:128] = small[:, 0:128]
    packed[0:128, 128:256] = jnp.broadcast_to(trace[0:1, :], (128, 128))
    packed[128:256, 128:256] = small[128:256, 128:256]
    packed[:, 256:384] = dot_split(split(cross[...]), parts, 1, 0).T


def sum_over_tok(pos, pieces, out):
    blocks = [pieces[8 * i : 8 * i + 8, :] for i in range(NX * NZ)]
    while len(blocks) > 1:
        blocks = [a + b for a, b in zip(blocks[0::2], blocks[1::2])]
    for i in range(NX * NZ):
        out[8 * i : 8 * i + 8, :] = blocks[0]


def keymap_body(width, pos, joined, out, reduced, li):
    scale = joined[0:1, 128:129] / width + eps
    row = lax.broadcasted_iota(jnp.int32, (256, 256), 0)
    col = lax.broadcasted_iota(jnp.int32, (256, 256), 1)
    identity = jnp.where(row == col, ridge, 0.0).astype(f32)
    reduced[...] = joined[:, 0:256] / scale + identity
    inverse_factor_256(reduced, li)
    rhs = joined[:, 256:384].T
    out[...] = dot(dot(rhs, li[...], 1, 1), li[...], 1, 0)


def place_body(pos, own, other, out):
    for j in range(NY):
        y = lax.rem(pos[2] + NY - j, NY)
        out[NCORE * y + pos[3]] = own[128 * j : 128 * j + 128, :]
        out[NCORE * y + (1 - pos[3])] = other[128 * j : 128 * j + 128, :]


def along_x(value, j):
    pairs = [(x * NZ + z, ((x + j) % NX) * NZ + z) for x in range(NX) for z in range(NZ)]
    return lax.ppermute(value, "tok", pairs)


def along_quad(value, j):
    pairs = [
        (x * NZ + z, x * NZ + z // NQ * NQ + (z + j) % NQ) for x in range(NX) for z in range(NZ)
    ]
    return lax.ppermute(value, "tok", pairs)


def other_quad(value):
    pairs = [(x * NZ + z, x * NZ + (z + NQ) % NZ) for x in range(NX) for z in range(NZ)]
    return lax.ppermute(value, "tok", pairs)


def along_y(value, j):
    pairs = [(y * NCORE + c, ((y + j) % NY) * NCORE + c) for y in range(NY) for c in range(NCORE)]
    return lax.ppermute(value, "head", pairs)


def other_core(value):
    pairs = [(y * NCORE + c, y * NCORE + 1 - c) for y in range(NY) for c in range(NCORE)]
    return lax.ppermute(value, "head", pairs)


def scatter(move, parts):
    return [parts[0]] + [move(parts[j], j) for j in range(1, 4)]


def gather(move, value):
    return [value] + [move(value, j) for j in range(1, 4)]


def on_device(queries, keys, basis):
    q, key, b = queries[:, 0, :], keys[:, 0, :], basis[0]
    width, rank = b.shape
    features = key.shape[1]
    total = q.shape[0] * lax.axis_size("tok")
    tok, head = lax.axis_index("tok"), lax.axis_index("head")
    pos = jnp.stack([tok // NZ, tok % NQ, head // NCORE, head % NCORE]).astype(jnp.int32)

    top, low, cross, trace, *quarters = products_call(pos, q, key, b, total)
    quarter, piece = (width // NX, rank), (width // NX // NQ, rank)
    arrived = scatter(along_x, quarters)
    pieces = call(sum_and_split, [piece] * NQ, [pltpu.VMEM(quarter, f32)], pos, *arrived)
    a0, a1, a2, a3 = scatter(along_quad, pieces)
    half = (a0 + a2) + (a1 + a3)
    whole = half + other_quad(half)
    rows = call(join, quarter, [], pos, *gather(along_quad, whole))

    square = pltpu.VMEM((rank, rank), f32)
    refined, packed = call(
        subspace_body,
        [(width, rank), (rank, rank + features)],
        [
            pltpu.VMEM((width, rank), f32), square, square,
            pltpu.VMEM((width, width), bf16), pltpu.VMEM((width, width), bf16),
            pltpu.SemaphoreType.DMA((2,)),
        ],
        pos, *gather(along_x, rows), cross, trace, far=(top, low),
    )
    pieces = lax.all_to_all(packed, "tok", 0, 0, tiled=True)
    sums = call(sum_over_tok, packed.shape, [], pos, pieces)
    joined = lax.all_to_all(sums, "tok", 0, 0, tiled=True)

    def keymap(*refs):
        keymap_body(width, *refs)

    mapped = call(keymap, (features, rank), [square, square], pos, joined)
    own = jnp.concatenate(gather(along_y, mapped), axis=0)
    every_map = call(
        place_body, (NY * NCORE, features, rank), [], pos, own, other_core(own)
    )
    return refined[None], every_map


def solution(mesh):
    placed = (P("tok", "head", None), P("tok", "head", None), P("head", None, None))
    return jax.shard_map(
        on_device,
        mesh=mesh,
        in_specs=placed,
        out_specs=(P("head", None, None), P()),
        check_vma=False,
    )
```

```python
import jax
import jax.numpy as jnp
from jax import lax
from jax.experimental import pallas as pl
from jax.experimental.pallas import tpu as pltpu
from jax.sharding import PartitionSpec as P

ridge = 0.1
eps = 1e-06
high = lax.Precision.HIGHEST
f32 = jnp.float32
bf16 = jnp.bfloat16

NX, NZ, NY, NCORE = 4, 8, 4, 2
NQ = 4
STEPS = 8

VMEM_LIMIT = 36 * 1024 * 1024


def dot(a, b, ca, cb, precision=high):
    return lax.dot_general(
        a, b, (((ca,), (cb,)), ((), ())), precision=precision, preferred_element_type=f32
    )


def split(v):
    top = v.astype(bf16)
    return top, (v - top.astype(f32)).astype(bf16)


def dot_split(a, b, ca, cb):
    (ah, al), (bh, bl) = a, b
    return dot(ah, bh, ca, cb, None) + (dot(ah, bl, ca, cb, None) + dot(al, bh, ca, cb, None))


def call(body, outs, scratch, pos, *args):
    spec = pl.BlockSpec(memory_space=pltpu.VMEM)
    many = isinstance(outs, list)
    shapes = [jax.ShapeDtypeStruct(s, f32) for s in (outs if many else [outs])]
    in_specs = [pl.BlockSpec(memory_space=pltpu.SMEM)] + [spec] * len(args)
    result = pl.pallas_call(
        body,
        out_shape=shapes,
        in_specs=in_specs,
        out_specs=[spec] * len(shapes),
        scratch_shapes=scratch,
        compiler_params=pltpu.CompilerParams(vmem_limit_bytes=VMEM_LIMIT),
    )(pos, *args)
    return result if many else result[0]


def inverse_factor_128(read, write):
    tile = (8, 128)
    row = lax.broadcasted_iota(jnp.int32, tile, 0)
    lane = lax.broadcasted_iota(jnp.int32, tile, 1)

    def lanes(v, j):
        return jnp.broadcast_to(v[:, j : j + 1], tile)

    def rows(v, i):
        return jnp.broadcast_to(v[i : i + 1, :], tile)

    def panels(turn, carry):
        left, right = list(carry[:16]), list(carry[16:])
        for p in range(STEPS):
            base = 8 * p
            cols = [lanes(left[p], base + j) for j in range(8)]
            s = [[rows(cols[j], i) for j in range(i + 1)] for i in range(8)]
            r = []
            for j in range(8):
                r.append(lax.rsqrt(s[j][j]))
                for i in range(j + 1, 8):
                    s[i][j] = s[i][j] * r[j]
                for i in range(j + 1, 8):
                    for l in range(j + 1, i + 1):
                        s[i][l] = s[i][l] - s[i][j] * s[l][j]

            def solve(v):
                for j in range(8):
                    v[j] = v[j] * r[j]
                    for i in range(j + 1, 8):
                        v[i] = v[i] - s[i][j] * v[j]
                return v

            ul = solve([rows(left[p], i) for i in range(8)])
            ur = solve([rows(right[p], i) for i in range(8)])
            out = ur[0]
            for i in range(1, 8):
                out = jnp.where(row == i, ur[i], out)
            write(turn * STEPS + p, out)
            for k in range(p + 1, 16):
                c = solve([lanes(left[k], base + j) for j in range(8)])
                for i in range(8):
                    left[k] = left[k] - c[i] * ul[i]
                    right[k] = right[k] - c[i] * ur[i]
        rest = [jnp.zeros(tile, f32)] * STEPS
        left = [pltpu.roll(v, 128 - 8 * STEPS, 1) for v in left[STEPS:]] + rest
        return tuple(left + right[STEPS:] + rest)

    left = [read(r) for r in range(16)]
    right = [jnp.where(lane == row + 8 * r, 1.0, 0.0).astype(f32) for r in range(16)]
    lax.fori_loop(0, 16 // STEPS, panels, tuple(left + right))


def inverse_factor_256(a_ref, li_ref):
    def half(h, carry):
        base = pl.multiple_of(h * 128, 128)

        @pl.when(h == 1)
        def _():
            l21 = dot(a_ref[128:256, 0:128], li_ref[0:128, 0:128], 1, 1)
            a_ref[128:256, 0:128] = l21
            a_ref[128:256, 128:256] = a_ref[128:256, 128:256] - dot(l21, l21, 1, 1)

        def part(r):
            return pl.ds(pl.multiple_of(base + 8 * r, 8), 8), pl.ds(base, 128)

        def write(r, v):
            li_ref[part(r)] = v

        inverse_factor_128(lambda r: a_ref[part(r)], write)
        return carry

    lax.fori_loop(0, 2, half, 0)
    li11, li22 = li_ref[0:128, 0:128], li_ref[128:256, 128:256]
    li_ref[128:256, 0:128] = -dot(li22, dot(a_ref[128:256, 0:128], li11, 1, 0), 1, 0)
    li_ref[0:128, 128:256] = jnp.zeros((128, 128), f32)


def products_call(pos, q, k, b, total):
    tokens, width = q.shape
    features, rank = k.shape[1], b.shape[1]
    tiles = [tokens // 8, tokens // 8, tokens // 4, tokens // 2]
    edges = [sum(tiles[:i]) for i in range(len(tiles) + 1)]
    count = len(tiles)
    side = width // 4
    spans = [slice(side * i, side * i + side) for i in range(4)]
    norm = 1.0 / total

    def body(pos, q_hbm, k_hbm, b_hbm, top, low, cross, trace, o0, o1, o2, o3,
             q, k, b, gram, sems):
        arrivals = []
        for i in range(count):
            part = pl.ds(edges[i], tiles[i])
            pair = [
                pltpu.make_async_copy(q_hbm.at[part], q.at[part], sems.at[2 * i]),
                pltpu.make_async_copy(k_hbm.at[part], k.at[part], sems.at[2 * i + 1]),
            ]
            for copy in pair:
                copy.start()
            arrivals.append(pair)
        basis_copy = pltpu.make_async_copy(b_hbm, b, sems.at[2 * count])
        basis_copy.start()
        for i in range(count):
            for copy in arrivals[i]:
                copy.wait()
            rows = slice(edges[i], edges[i + 1])
            for span in spans:
                part = dot(q[rows, span], q[rows, span.start:], 0, 0, None)
                gram[span, span.start:] = part if i == 0 else gram[span, span.start:] + part
            part = dot(k[rows, :], q[rows, :], 0, 0, None)
            cross[...] = part if i == 0 else cross[...] + part
        cross[...] = cross[...] * norm

        row = lax.broadcasted_iota(jnp.int32, (side, side), 0)
        col = lax.broadcasted_iota(jnp.int32, (side, side), 1)
        diagonal = jnp.zeros((side, side), f32)
        for i in range(4):
            for j in range(i, 4):
                block = gram[spans[i], spans[j]] * norm
                top[spans[i], spans[j]], low[spans[i], spans[j]] = split(block)
                if j == i:
                    diagonal = diagonal + jnp.where(row == col, block, 0.0)
                else:
                    top[spans[j], spans[i]], low[spans[j], spans[i]] = split(block.T)
        total_of = jnp.sum(jnp.sum(diagonal, axis=1, keepdims=True), axis=0, keepdims=True)
        trace[...] = jnp.broadcast_to(total_of, trace.shape)

        basis_copy.wait()
        basis = split(b[...])
        for j, out in enumerate((o0, o1, o2, o3)):
            part = pl.ds(pl.multiple_of(lax.rem(pos[0] + j, NX) * side, side), side)
            out[...] = dot_split((top[part, :], low[part, :]), basis, 1, 0)

    hbm = pl.BlockSpec(memory_space=pltpu.HBM)
    vmem = pl.BlockSpec(memory_space=pltpu.VMEM)
    shape = jax.ShapeDtypeStruct
    return pl.pallas_call(
        body,
        out_shape=[
            shape((width, width), bf16),
            shape((width, width), bf16),
            shape((features, width), f32),
            shape((8, 128), f32),
        ] + [shape((side, rank), f32)] * NX,
        in_specs=[pl.BlockSpec(memory_space=pltpu.SMEM), hbm, hbm, hbm],
        out_specs=[vmem] * (4 + NX),
        scratch_shapes=[
            pltpu.VMEM((tokens, width), bf16),
            pltpu.VMEM((tokens, features), bf16),
            pltpu.VMEM((width, rank), f32),
            pltpu.VMEM((width, width), f32),
            pltpu.SemaphoreType.DMA((2 * count + 1,)),
        ],
        compiler_params=pltpu.CompilerParams(vmem_limit_bytes=VMEM_LIMIT),
    )(pos, *[pltpu.with_memory_space_constraint(v, pltpu.HBM) for v in (q, k, b)])


def sum_and_split(pos, a0, a1, a2, a3, o0, o1, o2, o3, acc):
    acc[...] = (a0[...] + a2[...]) + (a1[...] + a3[...])
    size = acc.shape[0] // NQ
    for j, out in enumerate((o0, o1, o2, o3)):
        start = pl.multiple_of(lax.rem(pos[1] + j, NQ) * size, size)
        out[...] = acc[pl.ds(start, size), :]


def join(pos, a0, a1, a2, a3, out):
    size = a0.shape[0]
    for j, block in enumerate((a0, a1, a2, a3)):
        start = pl.multiple_of(lax.rem(pos[1] + NQ - j, NQ) * size, size)
        out[pl.ds(start, size), :] = block[...]


def subspace_body(pos, s0, s1, s2, s3, cross, trace, top, low, refined, packed, image, inner, li):
    size = s0.shape[0]
    for j, block in enumerate((s0, s1, s2, s3)):
        start = pl.multiple_of(lax.rem(pos[0] + NX - j, NX) * size, size)
        image[pl.ds(start, size), :] = block[...]
    inner[...] = dot(image[...], image[...], 0, 0)
    inverse_factor_256(inner, li)
    basis = dot(image[...], li[...], 1, 1)
    refined[...] = basis
    parts = split(basis)
    product = dot_split((top[...], low[...]), parts, 1, 0)
    small = dot_split(parts, split(product), 0, 0)
    packed[:, 0:128] = small[:, 0:128]
    packed[0:128, 128:256] = jnp.broadcast_to(trace[0:1, :], (128, 128))
    packed[128:256, 128:256] = small[128:256, 128:256]
    packed[:, 256:384] = dot_split(split(cross[...]), parts, 1, 0).T


def sum_over_tok(pos, pieces, out):
    blocks = [pieces[8 * i : 8 * i + 8, :] for i in range(NX * NZ)]
    while len(blocks) > 1:
        blocks = [a + b for a, b in zip(blocks[0::2], blocks[1::2])]
    for i in range(NX * NZ):
        out[8 * i : 8 * i + 8, :] = blocks[0]


def keymap_body(width, pos, joined, out, reduced, li):
    scale = joined[0:1, 128:129] / width + eps
    row = lax.broadcasted_iota(jnp.int32, (256, 256), 0)
    col = lax.broadcasted_iota(jnp.int32, (256, 256), 1)
    identity = jnp.where(row == col, ridge, 0.0).astype(f32)
    reduced[...] = joined[:, 0:256] / scale + identity
    inverse_factor_256(reduced, li)
    rhs = joined[:, 256:384].T
    out[...] = dot(dot(rhs, li[...], 1, 1), li[...], 1, 0)


def place_body(pos, own, other, out):
    for j in range(NY):
        y = lax.rem(pos[2] + NY - j, NY)
        out[NCORE * y + pos[3]] = own[128 * j : 128 * j + 128, :]
        out[NCORE * y + (1 - pos[3])] = other[128 * j : 128 * j + 128, :]


def along_x(value, j):
    pairs = [(x * NZ + z, ((x + j) % NX) * NZ + z) for x in range(NX) for z in range(NZ)]
    return lax.ppermute(value, "tok", pairs)


def along_quad(value, j):
    pairs = [
        (x * NZ + z, x * NZ + z // NQ * NQ + (z + j) % NQ) for x in range(NX) for z in range(NZ)
    ]
    return lax.ppermute(value, "tok", pairs)


def other_quad(value):
    pairs = [(x * NZ + z, x * NZ + (z + NQ) % NZ) for x in range(NX) for z in range(NZ)]
    return lax.ppermute(value, "tok", pairs)


def along_y(value, j):
    pairs = [(y * NCORE + c, ((y + j) % NY) * NCORE + c) for y in range(NY) for c in range(NCORE)]
    return lax.ppermute(value, "head", pairs)


def other_core(value):
    pairs = [(y * NCORE + c, y * NCORE + 1 - c) for y in range(NY) for c in range(NCORE)]
    return lax.ppermute(value, "head", pairs)


def scatter(move, parts):
    return [parts[0]] + [move(parts[j], j) for j in range(1, 4)]


def gather(move, value):
    return [value] + [move(value, j) for j in range(1, 4)]


def on_device(queries, keys, basis):
    q, key, b = queries[:, 0, :], keys[:, 0, :], basis[0]
    width, rank = b.shape
    features = key.shape[1]
    total = q.shape[0] * lax.axis_size("tok")
    tok, head = lax.axis_index("tok"), lax.axis_index("head")
    pos = jnp.stack([tok // NZ, tok % NQ, head // NCORE, head % NCORE]).astype(jnp.int32)

    top, low, cross, trace, *quarters = products_call(pos, q, key, b, total)
    quarter, piece = (width // NX, rank), (width // NX // NQ, rank)
    arrived = scatter(along_x, quarters)
    pieces = call(sum_and_split, [piece] * NQ, [pltpu.VMEM(quarter, f32)], pos, *arrived)
    a0, a1, a2, a3 = scatter(along_quad, pieces)
    half = (a0 + a2) + (a1 + a3)
    whole = half + other_quad(half)
    rows = call(join, quarter, [], pos, *gather(along_quad, whole))

    square = pltpu.VMEM((rank, rank), f32)
    refined, packed = call(
        subspace_body,
        [(width, rank), (rank, rank + features)],
        [pltpu.VMEM((width, rank), f32), square, square],
        pos, *gather(along_x, rows), cross, trace, top, low,
    )
    pieces = lax.all_to_all(packed, "tok", 0, 0, tiled=True)
    sums = call(sum_over_tok, packed.shape, [], pos, pieces)
    joined = lax.all_to_all(sums, "tok", 0, 0, tiled=True)

    def keymap(*refs):
        keymap_body(width, *refs)

    mapped = call(keymap, (features, rank), [square, square], pos, joined)
    own = jnp.concatenate(gather(along_y, mapped), axis=0)
    every_map = call(
        place_body, (NY * NCORE, features, rank), [], pos, own, other_core(own)
    )
    return refined[None], every_map


def solution(mesh):
    placed = (P("tok", "head", None), P("tok", "head", None), P("head", None, None))
    return jax.shard_map(
        on_device,
        mesh=mesh,
        in_specs=placed,
        out_specs=(P("head", None, None), P()),
        check_vma=False,
    )
```

```python
import jax
import jax.numpy as jnp
from jax import lax
from jax.experimental import pallas as pl
from jax.experimental.pallas import tpu as pltpu
from jax.sharding import Mesh, PartitionSpec as P

ridge = 0.1
eps = 1e-06
high = lax.Precision.HIGHEST
f32 = jnp.float32
bf16 = jnp.bfloat16

NX, NZ, NY, NCORE = 4, 8, 4, 2
NQ = 4

VMEM_LIMIT = 36 * 1024 * 1024


def dot(a, b, ca, cb, precision=high):
    return lax.dot_general(
        a, b, (((ca,), (cb,)), ((), ())), precision=precision, preferred_element_type=f32
    )


def split(v):
    top = v.astype(bf16)
    return top, (v - top.astype(f32)).astype(bf16)


def dot_split(a, b, ca, cb):
    (ah, al), (bh, bl) = a, b
    return dot(ah, bh, ca, cb, None) + (dot(ah, bl, ca, cb, None) + dot(al, bh, ca, cb, None))


def call(body, outs, scratch, pos, *args):
    spec = pl.BlockSpec(memory_space=pltpu.VMEM)
    many = isinstance(outs, list)
    shapes = [jax.ShapeDtypeStruct(s, f32) for s in (outs if many else [outs])]
    in_specs = [pl.BlockSpec(memory_space=pltpu.SMEM)] + [spec] * len(args)
    result = pl.pallas_call(
        body,
        out_shape=shapes,
        in_specs=in_specs,
        out_specs=[spec] * len(shapes),
        scratch_shapes=scratch,
        compiler_params=pltpu.CompilerParams(vmem_limit_bytes=VMEM_LIMIT),
    )(pos, *args)
    return result if many else result[0]


def inverse_factor_128(read, write, buf):
    tile = (8, 128)
    row = lax.broadcasted_iota(jnp.int32, tile, 0)
    lane = lax.broadcasted_iota(jnp.int32, tile, 1)

    def lanes(v, j):
        return jnp.broadcast_to(v[:, j : j + 1], tile)

    def rows(v, i):
        return jnp.broadcast_to(v[i : i + 1, :], tile)

    left = [read(r) for r in range(16)]
    right = [jnp.where(lane == row + 8 * r, 1.0, 0.0).astype(f32) for r in range(16)]
    for p in range(16):
        base, slot = 8 * p, 64 * (p % 2)
        for j in range(8):
            buf[slot + 8 * j : slot + 8 * j + 8, :] = lanes(left[p], base + j)
        s = [
            [buf[pl.ds(slot + 8 * j + i, 8, stride=0), :] for j in range(i + 1)]
            for i in range(8)
        ]
        r = []
        for j in range(8):
            r.append(lax.rsqrt(s[j][j]))
            for i in range(j + 1, 8):
                s[i][j] = s[i][j] * r[j]
            for i in range(j + 1, 8):
                for l in range(j + 1, i + 1):
                    s[i][l] = s[i][l] - s[i][j] * s[l][j]

        def solve(v):
            for j in range(8):
                v[j] = v[j] * r[j]
                for i in range(j + 1, 8):
                    v[i] = v[i] - s[i][j] * v[j]
            return v

        ul = solve([rows(left[p], i) for i in range(8)])
        ur = solve([rows(right[p], i) for i in range(8)])
        out = ur[0]
        for i in range(1, 8):
            out = jnp.where(row == i, ur[i], out)
        write(p, out)
        for k in range(p + 1, 16):
            c = solve([lanes(left[k], base + j) for j in range(8)])
            for i in range(8):
                left[k] = left[k] - c[i] * ul[i]
                right[k] = right[k] - c[i] * ur[i]


def inverse_factor_block(a_ref, li_ref, buf):
    def write(r, v):
        li_ref[8 * r : 8 * r + 8, :] = v

    inverse_factor_128(lambda r: a_ref[8 * r : 8 * r + 8, :], write, buf)


def inverse_factor_256(a_ref, li_ref, buf):
    def half(h, carry):
        base = pl.multiple_of(h * 128, 128)

        @pl.when(h == 1)
        def _():
            l21 = dot(a_ref[128:256, 0:128], li_ref[0:128, 0:128].T, 1, 0)
            a_ref[128:256, 0:128] = l21
            a_ref[128:256, 128:256] = a_ref[128:256, 128:256] - dot(l21, l21.T, 1, 0)

        def part(r):
            return pl.ds(pl.multiple_of(base + 8 * r, 8), 8), pl.ds(base, 128)

        def write(r, v):
            li_ref[part(r)] = v

        inverse_factor_128(lambda r: a_ref[part(r)], write, buf)
        return carry

    lax.fori_loop(0, 2, half, 0)
    li11, li22 = li_ref[0:128, 0:128], li_ref[128:256, 128:256]
    li_ref[128:256, 0:128] = -dot(li22, dot(a_ref[128:256, 0:128], li11, 1, 0), 1, 0)
    li_ref[0:128, 128:256] = jnp.zeros((128, 128), f32)


def products_call(pos, q, k, b, total):
    tokens, width = q.shape
    features, rank = k.shape[1], b.shape[1]
    tiles = [tokens // 8, tokens // 8, tokens // 4, tokens // 2]
    edges = [sum(tiles[:i]) for i in range(len(tiles) + 1)]
    count = len(tiles)
    side = width // 4
    spans = [slice(side * i, side * i + side) for i in range(4)]
    norm = 1.0 / total

    def body(pos, q_hbm, k_hbm, b_hbm, top, low, cross, trace, o0, o1, o2, o3,
             q, k, b, gram, sems):
        arrivals = []
        for i in range(count):
            part = pl.ds(edges[i], tiles[i])
            pair = [
                pltpu.make_async_copy(q_hbm.at[part], q.at[part], sems.at[2 * i]),
                pltpu.make_async_copy(k_hbm.at[part], k.at[part], sems.at[2 * i + 1]),
            ]
            for copy in pair:
                copy.start()
            arrivals.append(pair)
        basis_copy = pltpu.make_async_copy(b_hbm, b, sems.at[2 * count])
        basis_copy.start()
        for i in range(count):
            for copy in arrivals[i]:
                copy.wait()
            rows = slice(edges[i], edges[i + 1])
            for span in spans:
                part = dot(q[rows, span], q[rows, span.start:], 0, 0, None)
                gram[span, span.start:] = part if i == 0 else gram[span, span.start:] + part
            part = dot(k[rows, :], q[rows, :], 0, 0, None)
            cross[...] = part if i == 0 else cross[...] + part
        cross[...] = cross[...] * norm

        row = lax.broadcasted_iota(jnp.int32, (side, side), 0)
        col = lax.broadcasted_iota(jnp.int32, (side, side), 1)
        diagonal = jnp.zeros((side, side), f32)
        for i in range(4):
            for j in range(i, 4):
                block = gram[spans[i], spans[j]] * norm
                top[spans[i], spans[j]], low[spans[i], spans[j]] = split(block)
                if j == i:
                    diagonal = diagonal + jnp.where(row == col, block, 0.0)
                else:
                    top[spans[j], spans[i]], low[spans[j], spans[i]] = split(block.T)
        total_of = jnp.sum(jnp.sum(diagonal, axis=1, keepdims=True), axis=0, keepdims=True)
        trace[...] = jnp.broadcast_to(total_of, trace.shape)

        basis_copy.wait()
        basis = split(b[...])
        for j, out in enumerate((o0, o1, o2, o3)):
            part = pl.ds(pl.multiple_of(lax.rem(pos[0] + j, NX) * side, side), side)
            out[...] = dot_split((top[part, :], low[part, :]), basis, 1, 0)

    hbm = pl.BlockSpec(memory_space=pltpu.HBM)
    vmem = pl.BlockSpec(memory_space=pltpu.VMEM)
    shape = jax.ShapeDtypeStruct
    return pl.pallas_call(
        body,
        out_shape=[
            shape((width, width), bf16),
            shape((width, width), bf16),
            shape((features, width), f32),
            shape((8, 128), f32),
        ] + [shape((side, rank), f32)] * NX,
        in_specs=[pl.BlockSpec(memory_space=pltpu.SMEM), hbm, hbm, hbm],
        out_specs=[vmem] * (4 + NX),
        scratch_shapes=[
            pltpu.VMEM((tokens, width), bf16),
            pltpu.VMEM((tokens, features), bf16),
            pltpu.VMEM((width, rank), f32),
            pltpu.VMEM((width, width), f32),
            pltpu.SemaphoreType.DMA((2 * count + 1,)),
        ],
        compiler_params=pltpu.CompilerParams(vmem_limit_bytes=VMEM_LIMIT),
    )(pos, *[pltpu.with_memory_space_constraint(v, pltpu.HBM) for v in (q, k, b)])


def sum_and_split(pos, a0, a1, a2, a3, o0, o1, o2, o3, acc):
    acc[...] = (a0[...] + a2[...]) + (a1[...] + a3[...])
    size = acc.shape[0] // NQ
    for j, out in enumerate((o0, o1, o2, o3)):
        start = pl.multiple_of(lax.rem(pos[1] + j, NQ) * size, size)
        out[...] = acc[pl.ds(start, size), :]


def join(pos, a0, a1, a2, a3, left, right):
    size = a0.shape[0]
    for j, block in enumerate((a0, a1, a2, a3)):
        part = pl.ds(pl.multiple_of(lax.rem(pos[1] + NQ - j, NQ) * size, size), size)
        left[part, :] = block[:, 0:128]
        right[part, :] = block[:, 128:256]


def assemble(pos, quarters, image):
    size = quarters[0].shape[0]
    for j, block in enumerate(quarters):
        start = pl.multiple_of(lax.rem(pos[0] + NX - j, NX) * size, size)
        image[pl.ds(start, size), :] = block[...]


def first_half_body(pos, s0, s1, s2, s3, first, image, inner, li, buf):
    assemble(pos, (s0, s1, s2, s3), image)
    inner[...] = dot(image[...], image[...], 0, 0)
    inverse_factor_block(inner, li, buf)
    first[...] = dot(image[...], li[...].T, 1, 0)


def second_half_body(pos, s0, s1, s2, s3, first, cross, trace, top, low, refined, packed,
                     image, inner, li, buf):
    assemble(pos, (s0, s1, s2, s3), image)
    begin = first[...]
    end = image[...]
    l21 = dot(end, begin, 0, 0)
    inner[...] = dot(end, end, 0, 0) - dot(l21, l21.T, 1, 0)
    inverse_factor_block(inner, li, buf)
    refined[:, 0:128] = begin
    refined[:, 128:256] = dot(end - dot(begin, l21.T, 1, 0), li[...].T, 1, 0)
    parts = split(refined[...])
    product = dot_split((top[...], low[...]), parts, 1, 0)
    small = dot_split(parts, split(product), 0, 0)
    corner = corner_of(128)
    packed[0:128, :] = jnp.where(corner, trace[0:1, :], small[0:128, 0:128])
    packed[128:256, :] = small[128:256, 0:128]
    packed[256:384, :] = small[128:256, 128:256]
    rhs = dot_split(split(cross[...]), parts, 1, 0)
    packed[384:512, :] = rhs[:, 0:128]
    packed[512:640, :] = rhs[:, 128:256]


def corner_of(size):
    row = lax.broadcasted_iota(jnp.int32, (size, size), 0)
    col = lax.broadcasted_iota(jnp.int32, (size, size), 1)
    return (row == 0) & (col == size - 1)


def total_of(blocks):
    while len(blocks) > 1:
        blocks = [a + b for a, b in zip(blocks[0::2], blocks[1::2])]
    return blocks[0]


def sum_blocks(repeats):
    def body(pos, *refs):
        ins, out = refs[:-1], refs[-1]
        size = out.shape[0] // repeats
        blocks = [r[size * i : size * i + size, :] for r in ins for i in range(r.shape[0] // size)]
        total = total_of(blocks)
        for i in range(repeats):
            out[size * i : size * i + size, :] = total

    return body


def keymap_body(width, pos, joined, out, reduced, li, buf):
    scale = joined[0:1, 127:128] / width + eps
    first = jnp.where(corner_of(128), joined[127:128, 0:1], joined[0:128, :])
    row = lax.broadcasted_iota(jnp.int32, (128, 128), 0)
    col = lax.broadcasted_iota(jnp.int32, (128, 128), 1)
    identity = jnp.where(row == col, ridge, 0.0).astype(f32)
    reduced[0:128, 0:128] = first / scale + identity
    reduced[128:256, 0:128] = joined[128:256, :] / scale
    reduced[128:256, 128:256] = joined[256:384, :] / scale + identity
    inverse_factor_256(reduced, li, buf)
    turned = li[...].T
    mapped = dot(joined[384:512, :], turned[0:128, :], 1, 0)
    mapped = mapped + dot(joined[512:640, :], turned[128:256, :], 1, 0)
    out[...] = dot(mapped, li[...], 1, 0)


def place_call(pos, own, other, shape):
    rows = shape[1]

    def body(pos, own, other, out, sems):
        copies = []
        for j in range(NY):
            first = NCORE * lax.rem(pos[2] + NY - j, NY)
            part = pl.ds(rows * j, rows)
            for source, core in ((own, pos[3]), (other, 1 - pos[3])):
                sem = sems.at[len(copies)]
                copies.append(pltpu.make_async_copy(source.at[part], out.at[first + core], sem))
        for copy in copies:
            copy.start()
        for copy in copies:
            copy.wait()

    vmem = pl.BlockSpec(memory_space=pltpu.VMEM)
    return pl.pallas_call(
        body,
        out_shape=jax.ShapeDtypeStruct(shape, f32),
        in_specs=[pl.BlockSpec(memory_space=pltpu.SMEM), vmem, vmem],
        out_specs=pl.BlockSpec(memory_space=pltpu.HBM),
        scratch_shapes=[pltpu.SemaphoreType.DMA((NY * NCORE,))],
        compiler_params=pltpu.CompilerParams(vmem_limit_bytes=VMEM_LIMIT),
    )(pos, own, other)


def ring(axis, count):
    return [
        lambda value, j=j: lax.ppermute(value, axis, [(i, (i + j) % count) for i in range(count)])
        for j in range(1, count)
    ]


def quad():
    return [
        lambda value, j=j: lax.ppermute(
            value, "z", [(i, i // NQ * NQ + (i + j) % NQ) for i in range(NZ)]
        )
        for j in range(1, NQ)
    ]


def other_quad(value):
    return lax.ppermute(value, "z", [(i, (i + NQ) % NZ) for i in range(NZ)])


def scatter(moves, parts):
    return [parts[0]] + [move(part) for move, part in zip(moves, parts[1:])]


def gather(moves, value):
    return [value] + [move(value) for move in moves]


def exchange(value, axis):
    return lax.all_to_all(value, axis, 0, 0, tiled=True)


def on_device(queries, keys, basis):
    q, key, b = queries[:, 0, :], keys[:, 0, :], basis[0]
    width, rank = b.shape
    features = key.shape[1]
    total = q.shape[0] * NX * NZ
    z = lax.axis_index("z")
    place = [lax.axis_index("x"), z % NQ, lax.axis_index("y"), lax.axis_index("core")]
    pos = jnp.stack(place).astype(jnp.int32)

    def summed(shape, *arrays, repeats=1):
        return call(sum_blocks(repeats), shape, [], pos, *arrays)

    top, low, cross, trace, *quarters = products_call(pos, q, key, b, total)
    quarter, piece = (width // NX, rank), (width // NX // NQ, rank)
    arrived = scatter(ring("x", NX), quarters)
    pieces = call(sum_and_split, [piece] * NQ, [pltpu.VMEM(quarter, f32)], pos, *arrived)
    a0, a1, a2, a3 = scatter(quad(), pieces)
    half = (a0 + a2) + (a1 + a3)
    whole = half + other_quad(half)
    column = (width // NX, 128)
    left, right = call(join, [column] * 2, [], pos, *gather(quad(), whole))
    lefts, rights = gather(ring("x", NX), left), gather(ring("x", NX), right)

    block, half_image = pltpu.VMEM((128, 128), f32), pltpu.VMEM((width, 128), f32)
    scratch = [half_image, block, block, block]
    first = call(first_half_body, (width, 128), scratch, pos, *lefts)
    refined, packed = call(
        second_half_body,
        [(width, rank), (640, 128)],
        scratch,
        pos, *rights, first, cross, trace, top, low,
    )
    rows = summed((640 // NZ, 128), exchange(packed, "z"))
    a0, a1, a2, a3 = gather(ring("x", NX), rows)
    joined = exchange(summed(packed.shape, a0, a2, a1, a3, repeats=NZ), "z")

    def keymap(*refs):
        keymap_body(width, *refs)

    square = pltpu.VMEM((rank, rank), f32)
    mapped = call(keymap, (features, rank), [square, square, block], pos, joined)
    own = jnp.concatenate(gather(ring("y", NY), mapped), axis=0)
    other = lax.ppermute(own, "core", [(0, 1), (1, 0)])
    every_map = place_call(pos, own, other, (NY * NCORE, features, rank))
    return refined[None], every_map


def solution(mesh):
    chips = Mesh(mesh.devices.reshape(NX, NZ, NY, NCORE), ("x", "z", "y", "core"))
    tok, head = ("x", "z"), ("y", "core")
    placed = (P(tok, head, None), P(tok, head, None), P(head, None, None))
    return jax.shard_map(
        on_device,
        mesh=chips,
        in_specs=placed,
        out_specs=(P(head, None, None), P()),
        check_vma=False,
    )
```

```python
import jax
import jax.numpy as jnp
from jax import lax
from jax.experimental import pallas as pl
from jax.experimental.pallas import tpu as pltpu
from jax.sharding import PartitionSpec as P

ridge = 0.1
eps = 1e-06
high = lax.Precision.HIGHEST
f32 = jnp.float32
bf16 = jnp.bfloat16

NX, NZ, NY, NCORE = 4, 8, 4, 2
NQ = 4
STEPS = 8

VMEM_LIMIT = 36 * 1024 * 1024


def dot(a, b, ca, cb, precision=high):
    return lax.dot_general(
        a, b, (((ca,), (cb,)), ((), ())), precision=precision, preferred_element_type=f32
    )


def split(v):
    top = v.astype(bf16)
    return top, (v - top.astype(f32)).astype(bf16)


def dot_split(a, b, ca, cb):
    (ah, al), (bh, bl) = a, b
    return dot(ah, bh, ca, cb, None) + (dot(ah, bl, ca, cb, None) + dot(al, bh, ca, cb, None))


def call(body, outs, scratch, pos, *args):
    spec = pl.BlockSpec(memory_space=pltpu.VMEM)
    many = isinstance(outs, list)
    shapes = [jax.ShapeDtypeStruct(s, f32) for s in (outs if many else [outs])]
    in_specs = [pl.BlockSpec(memory_space=pltpu.SMEM)] + [spec] * len(args)
    result = pl.pallas_call(
        body,
        out_shape=shapes,
        in_specs=in_specs,
        out_specs=[spec] * len(shapes),
        scratch_shapes=scratch,
        compiler_params=pltpu.CompilerParams(vmem_limit_bytes=VMEM_LIMIT),
    )(pos, *args)
    return result if many else result[0]


def inverse_factor_128(read, write, buf):
    tile = (8, 128)
    row = lax.broadcasted_iota(jnp.int32, tile, 0)
    lane = lax.broadcasted_iota(jnp.int32, tile, 1)

    def lanes(v, j):
        return jnp.broadcast_to(v[:, j : j + 1], tile)

    def rows(v, i):
        return jnp.broadcast_to(v[i : i + 1, :], tile)

    def panels(turn, carry):
        left, right = list(carry[:16]), list(carry[16:])
        for p in range(STEPS):
            base = 8 * p
            slot = 64 * (p % 2)
            for j in range(8):
                buf[slot + 8 * j : slot + 8 * j + 8, :] = lanes(left[p], base + j)
            s = [
                [buf[pl.ds(slot + 8 * j + i, 8, stride=0), :] for j in range(i + 1)]
                for i in range(8)
            ]
            r = []
            for j in range(8):
                r.append(lax.rsqrt(s[j][j]))
                for i in range(j + 1, 8):
                    s[i][j] = s[i][j] * r[j]
                for i in range(j + 1, 8):
                    for l in range(j + 1, i + 1):
                        s[i][l] = s[i][l] - s[i][j] * s[l][j]

            def solve(v):
                for j in range(8):
                    v[j] = v[j] * r[j]
                    for i in range(j + 1, 8):
                        v[i] = v[i] - s[i][j] * v[j]
                return v

            ul = solve([rows(left[p], i) for i in range(8)])
            ur = solve([rows(right[p], i) for i in range(8)])
            out = ur[0]
            for i in range(1, 8):
                out = jnp.where(row == i, ur[i], out)
            write(turn * STEPS + p, out)
            for k in range(p + 1, 16):
                c = solve([lanes(left[k], base + j) for j in range(8)])
                for i in range(8):
                    left[k] = left[k] - c[i] * ul[i]
                    right[k] = right[k] - c[i] * ur[i]
        rest = [jnp.zeros(tile, f32)] * STEPS
        left = [pltpu.roll(v, 128 - 8 * STEPS, 1) for v in left[STEPS:]] + rest
        return tuple(left + right[STEPS:] + rest)

    left = [read(r) for r in range(16)]
    right = [jnp.where(lane == row + 8 * r, 1.0, 0.0).astype(f32) for r in range(16)]
    lax.fori_loop(0, 16 // STEPS, panels, tuple(left + right))


def inverse_factor_256(a_ref, li_ref, buf):
    def half(h, carry):
        base = pl.multiple_of(h * 128, 128)

        @pl.when(h == 1)
        def _():
            l21 = dot(a_ref[128:256, 0:128], li_ref[0:128, 0:128].T, 1, 0)
            a_ref[128:256, 0:128] = l21
            a_ref[128:256, 128:256] = a_ref[128:256, 128:256] - dot(l21, l21.T, 1, 0)

        def part(r):
            return pl.ds(pl.multiple_of(base + 8 * r, 8), 8), pl.ds(base, 128)

        def write(r, v):
            li_ref[part(r)] = v

        inverse_factor_128(lambda r: a_ref[part(r)], write, buf)
        return carry

    lax.fori_loop(0, 2, half, 0)
    li11, li22 = li_ref[0:128, 0:128], li_ref[128:256, 128:256]
    li_ref[128:256, 0:128] = -dot(li22, dot(a_ref[128:256, 0:128], li11, 1, 0), 1, 0)
    li_ref[0:128, 128:256] = jnp.zeros((128, 128), f32)


def products_call(pos, q, k, b, total):
    tokens, width = q.shape
    features, rank = k.shape[1], b.shape[1]
    tiles = [tokens // 8, tokens // 8, tokens // 4, tokens // 2]
    edges = [sum(tiles[:i]) for i in range(len(tiles) + 1)]
    count = len(tiles)
    side = width // 4
    spans = [slice(side * i, side * i + side) for i in range(4)]
    norm = 1.0 / total

    def body(pos, q_hbm, k_hbm, b_hbm, top, low, cross, trace, o0, o1, o2, o3,
             q, k, b, gram, sems):
        arrivals = []
        for i in range(count):
            part = pl.ds(edges[i], tiles[i])
            pair = [
                pltpu.make_async_copy(q_hbm.at[part], q.at[part], sems.at[2 * i]),
                pltpu.make_async_copy(k_hbm.at[part], k.at[part], sems.at[2 * i + 1]),
            ]
            for copy in pair:
                copy.start()
            arrivals.append(pair)
        basis_copy = pltpu.make_async_copy(b_hbm, b, sems.at[2 * count])
        basis_copy.start()
        for i in range(count):
            for copy in arrivals[i]:
                copy.wait()
            rows = slice(edges[i], edges[i + 1])
            for span in spans:
                part = dot(q[rows, span], q[rows, span.start:], 0, 0, None)
                gram[span, span.start:] = part if i == 0 else gram[span, span.start:] + part
            part = dot(k[rows, :], q[rows, :], 0, 0, None)
            cross[...] = part if i == 0 else cross[...] + part
        cross[...] = cross[...] * norm

        row = lax.broadcasted_iota(jnp.int32, (side, side), 0)
        col = lax.broadcasted_iota(jnp.int32, (side, side), 1)
        diagonal = jnp.zeros((side, side), f32)
        for i in range(4):
            for j in range(i, 4):
                block = gram[spans[i], spans[j]] * norm
                top[spans[i], spans[j]], low[spans[i], spans[j]] = split(block)
                if j == i:
                    diagonal = diagonal + jnp.where(row == col, block, 0.0)
                else:
                    top[spans[j], spans[i]], low[spans[j], spans[i]] = split(block.T)
        total_of = jnp.sum(jnp.sum(diagonal, axis=1, keepdims=True), axis=0, keepdims=True)
        trace[...] = jnp.broadcast_to(total_of, trace.shape)

        basis_copy.wait()
        basis = split(b[...])
        for j, out in enumerate((o0, o1, o2, o3)):
            part = pl.ds(pl.multiple_of(lax.rem(pos[0] + j, NX) * side, side), side)
            out[...] = dot_split((top[part, :], low[part, :]), basis, 1, 0)

    hbm = pl.BlockSpec(memory_space=pltpu.HBM)
    vmem = pl.BlockSpec(memory_space=pltpu.VMEM)
    shape = jax.ShapeDtypeStruct
    return pl.pallas_call(
        body,
        out_shape=[
            shape((width, width), bf16),
            shape((width, width), bf16),
            shape((features, width), f32),
            shape((8, 128), f32),
        ] + [shape((side, rank), f32)] * NX,
        in_specs=[pl.BlockSpec(memory_space=pltpu.SMEM), hbm, hbm, hbm],
        out_specs=[vmem] * (4 + NX),
        scratch_shapes=[
            pltpu.VMEM((tokens, width), bf16),
            pltpu.VMEM((tokens, features), bf16),
            pltpu.VMEM((width, rank), f32),
            pltpu.VMEM((width, width), f32),
            pltpu.SemaphoreType.DMA((2 * count + 1,)),
        ],
        compiler_params=pltpu.CompilerParams(vmem_limit_bytes=VMEM_LIMIT),
    )(pos, *[pltpu.with_memory_space_constraint(v, pltpu.HBM) for v in (q, k, b)])


def sum_and_split(pos, a0, a1, a2, a3, o0, o1, o2, o3, acc):
    acc[...] = (a0[...] + a2[...]) + (a1[...] + a3[...])
    size = acc.shape[0] // NQ
    for j, out in enumerate((o0, o1, o2, o3)):
        start = pl.multiple_of(lax.rem(pos[1] + j, NQ) * size, size)
        out[...] = acc[pl.ds(start, size), :]


def join(pos, a0, a1, a2, a3, out):
    size = a0.shape[0]
    for j, block in enumerate((a0, a1, a2, a3)):
        start = pl.multiple_of(lax.rem(pos[1] + NQ - j, NQ) * size, size)
        out[pl.ds(start, size), :] = block[...]


def subspace_body(pos, s0, s1, s2, s3, cross, trace, top, low, refined, packed, image, inner, li,
                  buf):
    size = s0.shape[0]
    for j, block in enumerate((s0, s1, s2, s3)):
        start = pl.multiple_of(lax.rem(pos[0] + NX - j, NX) * size, size)
        image[pl.ds(start, size), :] = block[...]
    inner[...] = dot(image[...], image[...], 0, 0)
    inverse_factor_256(inner, li, buf)
    basis = dot(image[...], li[...].T, 1, 0)
    refined[...] = basis
    parts = split(basis)
    product = dot_split((top[...], low[...]), parts, 1, 0)
    small = dot_split(parts, split(product), 0, 0)
    packed[:, 0:128] = small[:, 0:128]
    packed[0:128, 128:256] = jnp.broadcast_to(trace[0:1, :], (128, 128))
    packed[128:256, 128:256] = small[128:256, 128:256]
    packed[:, 256:384] = dot_split(split(cross[...]), parts, 1, 0).T


def sum_over_tok(pos, pieces, out):
    blocks = [pieces[8 * i : 8 * i + 8, :] for i in range(NX * NZ)]
    while len(blocks) > 1:
        blocks = [a + b for a, b in zip(blocks[0::2], blocks[1::2])]
    for i in range(NX * NZ):
        out[8 * i : 8 * i + 8, :] = blocks[0]


def keymap_body(width, pos, joined, out, reduced, li, buf):
    scale = joined[0:1, 128:129] / width + eps
    row = lax.broadcasted_iota(jnp.int32, (256, 256), 0)
    col = lax.broadcasted_iota(jnp.int32, (256, 256), 1)
    identity = jnp.where(row == col, ridge, 0.0).astype(f32)
    reduced[...] = joined[:, 0:256] / scale + identity
    inverse_factor_256(reduced, li, buf)
    rhs = joined[:, 256:384].T
    out[...] = dot(dot(rhs, li[...].T, 1, 0), li[...], 1, 0)


def place_body(pos, own, other, out):
    for j in range(NY):
        y = lax.rem(pos[2] + NY - j, NY)
        out[NCORE * y + pos[3]] = own[128 * j : 128 * j + 128, :]
        out[NCORE * y + (1 - pos[3])] = other[128 * j : 128 * j + 128, :]


def along_x(value, j):
    pairs = [(x * NZ + z, ((x + j) % NX) * NZ + z) for x in range(NX) for z in range(NZ)]
    return lax.ppermute(value, "tok", pairs)


def along_quad(value, j):
    pairs = [
        (x * NZ + z, x * NZ + z // NQ * NQ + (z + j) % NQ) for x in range(NX) for z in range(NZ)
    ]
    return lax.ppermute(value, "tok", pairs)


def other_quad(value):
    pairs = [(x * NZ + z, x * NZ + (z + NQ) % NZ) for x in range(NX) for z in range(NZ)]
    return lax.ppermute(value, "tok", pairs)


def along_y(value, j):
    pairs = [(y * NCORE + c, ((y + j) % NY) * NCORE + c) for y in range(NY) for c in range(NCORE)]
    return lax.ppermute(value, "head", pairs)


def other_core(value):
    pairs = [(y * NCORE + c, y * NCORE + 1 - c) for y in range(NY) for c in range(NCORE)]
    return lax.ppermute(value, "head", pairs)


def scatter(move, parts):
    return [parts[0]] + [move(parts[j], j) for j in range(1, 4)]


def gather(move, value):
    return [value] + [move(value, j) for j in range(1, 4)]


def on_device(queries, keys, basis):
    q, key, b = queries[:, 0, :], keys[:, 0, :], basis[0]
    width, rank = b.shape
    features = key.shape[1]
    total = q.shape[0] * lax.axis_size("tok")
    tok, head = lax.axis_index("tok"), lax.axis_index("head")
    pos = jnp.stack([tok // NZ, tok % NQ, head // NCORE, head % NCORE]).astype(jnp.int32)

    top, low, cross, trace, *quarters = products_call(pos, q, key, b, total)
    quarter, piece = (width // NX, rank), (width // NX // NQ, rank)
    arrived = scatter(along_x, quarters)
    pieces = call(sum_and_split, [piece] * NQ, [pltpu.VMEM(quarter, f32)], pos, *arrived)
    a0, a1, a2, a3 = scatter(along_quad, pieces)
    half = (a0 + a2) + (a1 + a3)
    whole = half + other_quad(half)
    rows = call(join, quarter, [], pos, *gather(along_quad, whole))

    square, spread = pltpu.VMEM((rank, rank), f32), pltpu.VMEM((128, 128), f32)
    refined, packed = call(
        subspace_body,
        [(width, rank), (rank, rank + features)],
        [pltpu.VMEM((width, rank), f32), square, square, spread],
        pos, *gather(along_x, rows), cross, trace, top, low,
    )
    pieces = lax.all_to_all(packed, "tok", 0, 0, tiled=True)
    sums = call(sum_over_tok, packed.shape, [], pos, pieces)
    joined = lax.all_to_all(sums, "tok", 0, 0, tiled=True)

    def keymap(*refs):
        keymap_body(width, *refs)

    mapped = call(keymap, (features, rank), [square, square, spread], pos, joined)
    own = jnp.concatenate(gather(along_y, mapped), axis=0)
    every_map = call(
        place_body, (NY * NCORE, features, rank), [], pos, own, other_core(own)
    )
    return refined[None], every_map


def solution(mesh):
    placed = (P("tok", "head", None), P("tok", "head", None), P("head", None, None))
    return jax.shard_map(
        on_device,
        mesh=mesh,
        in_specs=placed,
        out_specs=(P("head", None, None), P()),
        check_vma=False,
    )
```
